512 devices in a mesh: slab: 128 (over z, y, core), rock: 4 (over x).
Axes of the slice: x: 4, y: 4, z: 16, core: 2. Of those that a mesh axis runs over, the one named last changes fastest.
Arguments:
- strain: float32 [16384, 6, 2048], P('slab', None, 'rock'), may hold values from -6 to 6
- dest: int32 [2, 16384, 1], P(None, 'slab'), may hold values from 0 to 127; in each aligned block of 128 rows (0 to 127, 128 to 255, ..., all dimensions but the last counted through in order) at most 2 rows name the same one
- det_row: int32 [2, 16384], P(None, 'slab'), may hold values from 0 to 7
- dirs: float32 [2, 4, 6], replicated, may hold values from -2.5 to 2.5
- rock_angles: float32 [16], replicated, may hold values from -2 to 2
- resolution: bfloat16 [2048, 2048], P(None, 'rock'), may hold values from -0.125 to 0.125
Outputs:
- detector: float32 [2, 1024, 16, 2048], P(None, 'slab', None, 'rock')
The draws below stay inside these ranges and needn't reach their ends.
Inputs may be any that keep to these rules, and one draw needn't show every extreme that they name: `dest`: within the 128 tiles of one index of slab, at one angle, at most 2 tiles name the same owner, a bound that some block reaches.
All inputs are finite; a program needn't handle non-finite values.
Results may differ from the reference program's by a relative error of at most 0.0003.
Values sent between devices are 32-bit elements; how exact they have to be, the bound alone decides.
A program may use at most 128 MiB of HBM per device.

```python
import math
import jax
import jax.numpy as jnp
import numpy as np
from jax import lax

TILES_DEV = 128
PIX = 2048
DEPTH = 1
COMP = 6
QDIR = 4
RANG = 16
ROWS = 8
ANGLES = 2
CAP = 2
TILES = 16384
VOX = 2048
DROWS = 1024
N_SLAB = 128


def touch_ends(array, own_key, smallest, largest):
    longest = array.shape.index(max(array.shape))
    spots = []
    for shift in (0, 1):
        where = [jax.random.randint(jax.random.fold_in(own_key, axis), (), 0, length) for axis, length in enumerate(array.shape)]
        where[longest] = (where[longest] + shift) % array.shape[longest]
        spots.append(tuple(where))
    return array.at[spots[0]].set(smallest).at[spots[1]].set(largest)


def block_scale(rng, extent, split, low, largest):
    def one(dim, blocks):
        heights = jax.random.uniform(jax.random.fold_in(jax.random.fold_in(rng, 6), dim), (blocks,), jnp.float32, low / len(split), largest / len(split))
        return jnp.repeat(jnp.exp(heights), extent[dim] // blocks).reshape((-1,) + (1,) * (len(extent) - dim - 1))

    factor_of = one(*split[0])
    for cut in split[1:]:
        factor_of = factor_of * one(*cut)
    return factor_of


def assign_block(rng, own, number, rows, number_of, top, bound, skew):
    ranking = jax.random.permutation(rng, number_of)
    crowded, usual = load_shares(number_of, rows * top, bound, skew, True), load_shares(number_of, rows * top, bound, skew, False)
    places = jnp.arange(number_of)

    def named(tallies, turn):
        used = int((tallies > 0).sum())
        fixed = max(1, used // 4)
        moved = fixed + (places - fixed + turn * (used - fixed)) % max(1, number_of - fixed)
        return jnp.zeros((number_of,), jnp.int32).at[ranking[jnp.where(places < fixed, places, moved)]].set(jnp.asarray(tallies, jnp.int32))

    tallies = jnp.where(number % 4 == 0, named(crowded, number // 4), named(usual, number - number // 4 - 1))
    mixed = jax.random.permutation(jax.random.fold_in(own, 3), number_of)
    donor, receiver = mixed[0:number_of // 2 * 2:2], mixed[1:number_of // 2 * 2:2]
    room = jnp.minimum(tallies[donor] - 1, bound - tallies[receiver]) // 2
    room = jnp.where((donor == ranking[0]) | (receiver == ranking[0]) | (tallies[receiver] == 0), 0, jnp.maximum(room, 0))
    moved = jax.random.randint(jax.random.fold_in(own, 4), (number_of // 2,), 0, 1 << 20) % (room + 1)
    tallies = tallies.at[donor].add(-moved).at[receiver].add(moved)
    items = jnp.searchsorted(jnp.cumsum(tallies), jnp.arange(rows * top), side="right").astype(jnp.int32)
    table = items.reshape(top, rows).T
    table = table[jax.random.permutation(jax.random.fold_in(own, 1), rows)]
    turn = jax.random.randint(jax.random.fold_in(own, 2), (rows, 1), 0, top)
    return jnp.take_along_axis(table, (jnp.arange(top)[None, :] + turn) % top, axis=1)


def load_shares(amount, total, limit, skew, full):
    portions = [(1 << 20) // math.isqrt(rank ** skew) + 1 for rank in range(1, amount + 1)]
    largest = limit if full else min(limit, max(-(-total // amount), total * portions[0] // sum(portions)))
    least = 1 if total - largest >= amount - 1 else 0
    holding, spare = [largest] + [least] * (amount - 1), total - largest - least * (amount - 1)
    while spare > 0:
        movable = [i for i in range(1, amount) if holding[i] < largest] or [i for i in range(1, amount) if holding[i] < limit]
        whole, budget = sum([portions[i] for i in movable]), spare
        for i in movable:
            more = min(limit - holding[i], max(1, budget * portions[i] // whole), spare)
            holding[i] = holding[i] + more
            spare = spare - more
    return np.array(holding)


def gaussian(rng, dims, width, most, cuts=(), dtype=jnp.bfloat16):
    values = width * jax.random.normal(rng, dims, jnp.float32)
    if cuts:
        values = values * block_scale(rng, dims, cuts, -0.22, 0.18)
    return jnp.clip(values, -most, most).astype(dtype)


def setup_inputs(seed: int = 0) -> dict:
    key_of = jax.random.split(jax.random.key(seed), 7)
    strain = gaussian(key_of[0], (TILES, COMP, VOX), 1.0, 6.0, ((0, 128), (2, 4)), jnp.float32)
    dest_keys = jax.random.split(jax.random.fold_in(key_of[1], 1), ANGLES * TILES // TILES_DEV)
    dest_turns = jax.random.permutation(jax.random.fold_in(key_of[1], 3), ANGLES * TILES // TILES_DEV)
    dest = jax.vmap(lambda own, number: assign_block(jax.random.fold_in(key_of[1], 2), own, number, TILES_DEV, N_SLAB, 1, CAP, 2))(dest_keys, dest_turns).reshape((ANGLES, TILES, 1))
    det_row = touch_ends(jax.random.randint(key_of[2], (ANGLES, TILES), 0, ROWS), jax.random.fold_in(key_of[2], 1), 0, ROWS - 1).astype(jnp.int32)
    dirs = gaussian(key_of[3], (ANGLES, QDIR, COMP), COMP ** -0.5, 2.5, (), jnp.float32)
    rock_angles = jnp.clip(jax.random.uniform(key_of[4], (RANG,), jnp.float32, -2.0, 2.0), -2.0, 2.0)
    resolution = gaussian(key_of[5], (PIX, PIX), PIX ** -0.5, 0.125, ((1, 4),))
    return dict(strain=strain, dest=dest, det_row=det_row, dirs=dirs, rock_angles=rock_angles, resolution=resolution)


def reference(strain, dest, det_row, dirs, rock_angles, resolution):
    norm = ROWS / (QDIR * DEPTH * TILES_DEV)
    blocks = strain.reshape(N_SLAB, TILES_DEV, COMP, VOX)
    spread = resolution.astype(jnp.float32)
    outputs = []
    for angle in range(ANGLES):
        target = (dest[angle, :, 0] * ROWS + det_row[angle]).astype(jnp.int32).reshape(N_SLAB, TILES_DEV)
        weights = dirs[angle]

        def step(carry, item):
            block, where = item
            proj = jnp.einsum("qc,tcv->tqv", weights, block, precision=lax.Precision.HIGHEST)
            expo = jnp.exp(-0.5 * (proj[:, :, None, :] - rock_angles[None, None, :, None]) ** 2)
            inten = jnp.sum(expo, axis=1).reshape(TILES_DEV, RANG, PIX, DEPTH).sum(axis=3)
            added = carry.at[where].add(inten.reshape(TILES_DEV, RANG * PIX))
            return added, None

        image, unused = lax.scan(step, jnp.zeros((DROWS, RANG * PIX), jnp.float32), (blocks, target))
        image = image.reshape(DROWS, RANG, PIX) * norm
        outputs.append(jnp.einsum("grp,pk->grk", image, spread, precision=lax.Precision.HIGHEST))
    return jnp.stack(outputs, axis=0)
```

```python
import functools
import math

import jax
import jax.numpy as jnp
from jax import lax
from jax.experimental import pallas as pl
from jax.experimental.pallas import tpu as pltpu
from jax.sharding import PartitionSpec as P

TILES_DEV = 128
DEPTH = 1
QDIR = 4
ROWS = 8
ANGLES = 2
CAP = 2
PLANE = 8
GROUPS = 4
MESH = pl.DeviceIdType.MESH


def kernel(
    nz, nd, nx,
    idx, cr, post, w, strain, res, oh, out,
    ysend, yrecv, ohrecv, ohm, zfirst, zrecv, ximg,
    oh_ss, oh_rs, y_ss, y_rs, z_ss, z_rs, x_ss, x_rs,
):
    me = lax.axis_index("slab")
    x = lax.axis_index("rock")
    z = lax.div(me, nd)
    d = lax.rem(me, nd)
    half = nz // 2
    owners = nz * nd
    px = strain.shape[2]
    per = zfirst.shape[2]
    lanes = w.shape[3]

    def plane(k):
        return {"slab": z * nd + lax.rem(d + k, nd)}

    def ring(step):
        return {"slab": lax.rem(z + step + nz, nz) * nd + d}

    def across(k):
        return {"rock": lax.rem(x + k, nx)}

    peers = [plane(k) for k in range(1, nd)] + [ring(1), ring(-1)] + [across(k) for k in range(1, nx)]
    barrier = pltpu.get_barrier_semaphore()
    for peer in peers:
        pl.semaphore_signal(barrier, inc=1, device_id=peer, device_id_type=MESH)
    pl.semaphore_wait(barrier, len(peers))

    def remote(src, dst, ss, rs, peer):
        return pltpu.make_async_remote_copy(
            src_ref=src, dst_ref=dst, send_sem=ss, recv_sem=rs, device_id=peer, device_id_type=MESH
        )

    def wait_bytes(ref, sem):
        pltpu.make_async_copy(ref, ref, sem).wait()

    def dest_z(m, sign):
        off = half - m
        if sign == 0:
            return lax.rem(z + off, nz)
        back = lax.rem(off, half)
        return lax.rem(z - back + nz, nz)

    for k in range(1, nd):
        remote(oh.at[lax.rem(d + k, nd)], ohrecv.at[d], oh_ss, oh_rs, plane(k)).start()
    ohrecv[d] = oh[d]

    upper = lax.broadcasted_iota(jnp.int32, (2 * QDIR, lanes), 0) < QDIR

    def pair(a, owner, put):
        base = (a * owners + owner) * CAP
        first, second = idx[base], idx[base + 1]
        for lb in range(px // lanes):
            cols = pl.ds(lb * lanes, lanes)
            total = None
            for c in range(w.shape[1]):
                s0 = jnp.broadcast_to(strain[first, pl.ds(c, 1), cols], upper.shape)
                s1 = jnp.broadcast_to(strain[second, pl.ds(c, 1), cols], upper.shape)
                term = w[a, c] * jnp.where(upper, s0, s1)
                total = term if total is None else total + term
            put(cols, total)

    def send_group(a, m):
        def one(k, carry):
            dk = lax.rem(d + k, nd)
            for sign in range(2):
                owner = dest_z(m, sign) * nd + dk

                def put(cols, value, sign=sign):
                    ysend[a, m, k - 1, sign, :, cols] = value

                pair(a, owner, put)
            remote(
                ysend.at[a, m, k - 1], yrecv.at[a, m, d], y_ss.at[a, m], y_rs.at[a, m], plane(k)
            ).start()
            return carry

        lax.fori_loop(1, nd, one, 0)
        for sign in range(2):

            def put(cols, value, sign=sign):
                yrecv[a, m, d, sign, :, cols] = value

            pair(a, dest_z(m, sign) * nd + d, put)

    def need_group(a, m):
        wait_bytes(yrecv.at[a, m, pl.ds(0, nd - 1)], y_rs.at[a, m])

    def work(a, m, sign, r):
        zd = dest_z(m, sign)
        p = yrecv[a, m, :, sign].reshape(nd * 2 * QDIR, px)
        e = jnp.exp2(p * (cr[r] - p))
        hi = e.astype(jnp.bfloat16)
        lo = (e - hi.astype(jnp.float32)).astype(jnp.bfloat16)
        lhs = ohm[a, pl.ds(pl.multiple_of(zd * ROWS, ROWS), ROWS), :].astype(jnp.bfloat16)
        return jnp.dot(lhs, jnp.concatenate([hi, lo], axis=0), preferred_element_type=jnp.float32)

    def z_step(a, m, g, way, has):
        here = zrecv.at[a, m - 1, way, g]
        if has:
            wait_bytes(here, z_rs.at[a, m - 1, way, g])

        def one(i, carry):
            value = work(a, m, way, g * per + i)
            if has:
                value = value + here[i]
            here[i] = value
            return carry

        lax.fori_loop(0, per, one, 0)
        remote(
            here, zrecv.at[a, m, way, g], z_ss.at[a, m, way, g], z_rs.at[a, m, way, g], ring(1 - 2 * way)
        ).start()

    def z_first(a):
        for way in range(2):

            def go(g, carry):
                def one(i, inner):
                    zfirst[a, g, i] = work(a, 0, 0, g * per + i)
                    return inner

                lax.fori_loop(0, per, one, 0)
                remote(
                    zfirst.at[a, g], zrecv.at[a, 0, way, g], z_ss.at[a, 0, way, g], z_rs.at[a, 0, way, g],
                    ring(1 - 2 * way),
                ).start()
                return carry

            lax.fori_loop(way * GROUPS // 2, (way + 1) * GROUPS // 2, go, 0)

    def z_second(a):
        for has in (True, False):

            def go(i, carry):
                for way in range(2):
                    g = i + (way if has else 1 - way) * (GROUPS // 2)
                    z_step(a, 1, g, way, has)
                return carry

            lax.fori_loop(0, GROUPS // 2, go, 0)

    def z_rest(a, m):
        def go(g, carry):
            for way in range(2):
                z_step(a, m, g, way, True)
            return carry

        lax.fori_loop(0, GROUPS, go, 0)

    def finish(a):
        def go(g, carry):
            for way in range(2):
                wait_bytes(zrecv.at[a, half - 1, way, g], z_rs.at[a, half - 1, way, g])

            def one(i, inner):
                r = g * per + i
                value = work(a, 0, 1, r) + zrecv[a, half - 1, 0, g, i] + zrecv[a, half - 1, 1, g, i]
                ximg[a, g, x, i] = value * post[r]
                return inner

            lax.fori_loop(0, per, one, 0)
            for k in range(1, nx):
                remote(ximg.at[a, g, x], ximg.at[a, g, x], x_ss.at[a, g], x_rs.at[a, g], across(k)).start()
            return carry

        lax.fori_loop(0, GROUPS, go, 0)

    def resolve(a):
        def go(g, carry):
            wait_bytes(ximg.at[a, g, pl.ds(0, nx - 1)], x_rs.at[a, g])
            total = None
            for j in range(nx):
                image = ximg[a, g, j].reshape(per * ROWS, px)
                hi = image.astype(jnp.bfloat16)
                lo = (image - hi.astype(jnp.float32)).astype(jnp.bfloat16)
                both = jnp.dot(
                    jnp.concatenate([hi, lo], axis=0), res[pl.ds(j * px, px), :], preferred_element_type=jnp.float32
                )
                part = both[: per * ROWS] + both[per * ROWS :]
                total = part if total is None else total + part
            out[a, pl.ds(g * per, per)] = total.reshape(per, ROWS, res.shape[1])
            return carry

        lax.fori_loop(0, GROUPS, go, 0)

    lead = 2
    units = [(a, m) for a in range(ANGLES) for m in range(half)]
    for a, m in units[:lead]:
        send_group(a, m)
    wait_bytes(ohrecv.at[pl.ds(0, nd - 1)], oh_rs)
    for a in range(ANGLES):
        columns = ohrecv[:, a].reshape(nd * 2 * QDIR, nz * ROWS)
        rows = columns.T
        ohm[a] = jnp.concatenate([rows, rows], axis=1)

    def steady(a):
        def go(m, carry):
            ahead = a * half + m + lead
            @pl.when(ahead < ANGLES * half)
            def _():
                send_group(lax.div(ahead, half), lax.rem(ahead, half))
            need_group(a, m)
            z_rest(a, m)
            return carry

        return go

    for a in range(ANGLES):
        for m in range(2):
            ahead = a * half + m + lead
            if ahead < ANGLES * half:
                send_group(ahead // half, ahead % half)
            need_group(a, m)
            (z_first if m == 0 else z_second)(a)
        if a > 0:
            finish(a - 1)
        if half > 2:
            lax.fori_loop(2, half, steady(a), 0)
        if a > 0:
            resolve(a - 1)
    finish(ANGLES - 1)
    resolve(ANGLES - 1)

    wait_bytes(ohrecv.at[pl.ds(0, nd - 1)], oh_ss)
    for a in range(ANGLES):

        def drain(m, carry):
            wait_bytes(ysend.at[a, m, pl.ds(0, nd - 1)], y_ss.at[a, m])
            return carry

        lax.fori_loop(0, half, drain, 0)

        def drain_z(m, carry):
            for way in range(2):
                for g in range(GROUPS):
                    wait_bytes(zrecv.at[a, m, way, g], z_ss.at[a, m, way, g])
            return carry

        for way in range(2):
            for g in range(way * GROUPS // 2, (way + 1) * GROUPS // 2):
                wait_bytes(zrecv.at[a, 0, way, g], z_ss.at[a, 0, way, g])
        lax.fori_loop(1, half, drain_z, 0)
        for g in range(GROUPS):
            wait_bytes(ximg.at[a, g, pl.ds(0, nx - 1)], x_ss.at[a, g])


def local(plane, strain, dest, det_row, dirs, rock_angles, resolution):
    nslab, nx = lax.axis_size("slab"), lax.axis_size("rock")
    nd, nz = plane, nslab // plane
    half = nz // 2
    tiles, comps, px = strain.shape
    out_px = resolution.shape[1]
    rocks = rock_angles.shape[0]
    per = rocks // GROUPS
    lanes = min(128, px)
    norm = ROWS / (QDIR * DEPTH * TILES_DEV)
    scale = math.sqrt(0.5 * math.log2(math.e))

    key = jnp.arange(tiles, dtype=jnp.int32)[None, :] * ROWS + det_row
    match = dest == jnp.arange(nslab, dtype=jnp.int32)[None, None, :]
    lowest = jnp.min(jnp.where(match, key[:, :, None], tiles * ROWS), axis=1)
    highest = jnp.max(jnp.where(match, key[:, :, None], -1), axis=1)
    keys = jnp.stack([jnp.where(highest >= 0, lowest, -1), jnp.where(highest > lowest, highest, -1)], axis=-1)
    idx = jnp.maximum(keys, 0) // ROWS
    rows = jnp.where(keys >= 0, keys % ROWS, -1)
    rows = jnp.transpose(rows.reshape(ANGLES, nz, nd, CAP), (2, 0, 3, 1))
    hot = rows[:, :, :, None, :, None] == jnp.arange(ROWS, dtype=jnp.int32)
    oh = jnp.broadcast_to(hot, (nd, ANGLES, CAP, QDIR, nz, ROWS)).astype(jnp.float32)
    oh = oh.reshape(nd, ANGLES, CAP * QDIR, nz * ROWS)

    w = jnp.transpose(dirs, (0, 2, 1)) * scale
    w = jnp.concatenate([w, w], axis=2)
    w = jnp.broadcast_to(w[..., None], (ANGLES, comps, 2 * QDIR, lanes))
    angles = rock_angles * scale
    cr = 2.0 * angles
    post = norm * jnp.exp2(-angles * angles)

    smem = pl.BlockSpec(memory_space=pltpu.SMEM)
    vmem = pl.BlockSpec(memory_space=pltpu.VMEM)
    dma = pltpu.SemaphoreType.DMA
    f32 = jnp.float32
    image = (per, ROWS, px)
    resolved = pl.pallas_call(
        functools.partial(kernel, nz, nd, nx),
        out_shape=jax.ShapeDtypeStruct((ANGLES, rocks, ROWS, out_px), f32),
        in_specs=[smem, smem, smem, vmem, vmem, vmem, vmem],
        out_specs=vmem,
        scratch_shapes=[
            pltpu.VMEM((ANGLES, half, nd - 1, 2, 2 * QDIR, px), f32),
            pltpu.VMEM((ANGLES, half, nd, 2, 2 * QDIR, px), f32),
            pltpu.VMEM((nd, ANGLES, CAP * QDIR, nz * ROWS), f32),
            pltpu.VMEM((ANGLES, nz * ROWS, 2 * nd * 2 * QDIR), f32),
            pltpu.VMEM((ANGLES, GROUPS, *image), f32),
            pltpu.VMEM((ANGLES, half, 2, GROUPS, *image), f32),
            pltpu.VMEM((ANGLES, GROUPS, nx, *image), f32),
            dma,
            dma,
            dma((ANGLES, half)),
            dma((ANGLES, half)),
            dma((ANGLES, half, 2, GROUPS)),
            dma((ANGLES, half, 2, GROUPS)),
            dma((ANGLES, GROUPS)),
            dma((ANGLES, GROUPS)),
        ],
        compiler_params=pltpu.CompilerParams(collective_id=0, has_side_effects=True),
    )(idx.reshape(-1), cr, post, w, strain, resolution, oh)
    return jnp.swapaxes(resolved, 1, 2)


def solution(mesh):
    placed = (
        P("slab", None, "rock"),
        P(None, "slab", None),
        P(None, "slab"),
        P(),
        P(),
        P(None, "rock"),
    )
    return jax.shard_map(
        functools.partial(local, PLANE),
        mesh=mesh,
        in_specs=placed,
        out_specs=P(None, "slab", None, "rock"),
        check_vma=False,
    )
```

```python
import functools
import math

import jax
import jax.numpy as jnp
from jax import lax
from jax.experimental import pallas as pl
from jax.experimental.pallas import tpu as pltpu
from jax.sharding import PartitionSpec as P

TILES_DEV = 128
DEPTH = 1
QDIR = 4
ROWS = 8
ANGLES = 2
CAP = 2
PLANE = 8
GROUPS = 4
LEAD = 3
MESH = pl.DeviceIdType.MESH


def kernel(
    nz, nd, norm,
    ra, dirs, dest, det_row, strain_hbm, res_hbm, out,
    idx, idx_v, w, strain, res, oh, ysend, yrecv, ohrecv, ohm, zfirst, zrecv, ximg,
    load_s, idx_s, oh_ss, oh_rs, y_ss, y_rs, z_ss, z_rs, x_ss, x_rs,
):
    me = lax.axis_index("slab")
    x = lax.axis_index("rock")
    nx = 4
    z = lax.div(me, nd)
    d = lax.rem(me, nd)
    half = nz // 2
    owners = nz * nd
    comps, blocks, tiles, lanes = strain.shape
    px = blocks * lanes
    per = zfirst.shape[2]
    scale = math.sqrt(0.5 * math.log2(math.e))
    f32, i32, bf16 = jnp.float32, jnp.int32, jnp.bfloat16

    def plane(k):
        return {"slab": z * nd + lax.rem(d + k, nd)}

    def ring(step):
        return {"slab": lax.rem(z + step + nz, nz) * nd + d}

    def across(k):
        return {"rock": lax.rem(x + k + nx, nx)}

    def remote(src, dst, ss, rs, peer):
        return pltpu.make_async_remote_copy(
            src_ref=src, dst_ref=dst, send_sem=ss, recv_sem=rs, device_id=peer, device_id_type=MESH
        )

    def wait_bytes(ref, sem):
        pltpu.make_async_copy(ref, ref, sem).wait()

    peers = [plane(k) for k in range(1, nd)] + [ring(1), ring(-1), across(1), across(-1)]
    barrier = pltpu.get_barrier_semaphore()
    for peer in peers:
        pl.semaphore_signal(barrier, inc=1, device_id=peer, device_id_type=MESH)

    loads = [
        pltpu.make_async_copy(
            strain_hbm.at[c, :, pl.ds(lb * lanes, lanes)], strain.at[c, lb], load_s.at[c * blocks + lb]
        )
        for c in range(comps)
        for lb in range(blocks)
    ]
    for load in loads:
        load.start()
    load_res = pltpu.make_async_copy(res_hbm, res, load_s.at[comps * blocks])
    load_res.start()

    upper = lax.broadcasted_iota(i32, (2 * QDIR, lanes), 0) < QDIR
    upper_rows = lax.broadcasted_iota(i32, (2 * QDIR, owners), 0) < QDIR
    number = lax.broadcasted_iota(i32, (tiles, owners), 0)
    owner_of = lax.broadcasted_iota(i32, (tiles, owners), 1)
    slot_rows = []
    for a in range(ANGLES):
        named = jnp.broadcast_to(dest[pl.ds(a, 1), :].astype(f32), (owners, tiles)).T.astype(i32)
        falls = jnp.broadcast_to(det_row[pl.ds(a, 1), :].astype(f32), (owners, tiles)).T.astype(i32)
        key = number * ROWS + falls
        match = named == owner_of
        low = jnp.min(jnp.where(match, key, tiles * ROWS), axis=0, keepdims=True)
        high = jnp.max(jnp.where(match, key, -1), axis=0, keepdims=True)
        low = jnp.where(high >= 0, low, -1)
        high = jnp.where(high > low, high, -1)
        for slot, keys in enumerate((low, high)):
            idx_v[pl.ds(a * CAP + slot, 1), :] = lax.shift_right_logical(jnp.maximum(keys, 0), 3)
        low, high = [jnp.where(keys >= 0, keys & (ROWS - 1), -1).astype(f32) for keys in (low, high)]
        slot_rows.append(
            jnp.where(upper_rows, jnp.broadcast_to(low, upper_rows.shape), jnp.broadcast_to(high, upper_rows.shape))
        )
    idx_copy = pltpu.make_async_copy(idx_v, idx, idx_s)
    idx_copy.start()
    slot_rows = jnp.concatenate(slot_rows, axis=0).astype(bf16)
    source = lax.broadcasted_iota(i32, (owners, nz * ROWS), 0)
    target = lax.broadcasted_iota(i32, (owners, nz * ROWS), 1)
    row_of = (lax.broadcasted_iota(i32, (2 * ANGLES * QDIR, nz * ROWS), 1) & (ROWS - 1)).astype(f32)
    start_of = lax.shift_right_logical(target, 3) * nd
    for k in range(nd):
        spread = jnp.where(source == start_of + k, 1.0, 0.0).astype(bf16)
        there = jnp.dot(slot_rows, spread, preferred_element_type=f32)
        hot = jnp.where(there == row_of, 1.0, 0.0)
        for a in range(ANGLES):
            oh[k, a] = hot[a * 2 * QDIR : (a + 1) * 2 * QDIR]
    qs = lax.broadcasted_iota(i32, (2 * QDIR, lanes), 0) & (QDIR - 1)
    for a in range(ANGLES):
        for c in range(comps):
            column = jnp.full(qs.shape, dirs[a, 0, c])
            for q in range(1, QDIR):
                column = jnp.where(qs == q, dirs[a, q, c], column)
            w[a, c] = column * scale
    idx_copy.wait()
    for load in loads:
        load.wait()

    def dest_z(m, sign):
        off = half - m
        if sign == 0:
            return lax.rem(z + off, nz)
        back = lax.rem(off, half)
        return lax.rem(z - back + nz, nz)

    pl.semaphore_wait(barrier, len(peers))

    for k in range(1, nd):
        remote(oh.at[lax.rem(d + k, nd)], ohrecv.at[d], oh_ss, oh_rs, plane(k)).start()
    ohrecv[d] = oh[d]

    def pair(a, owner):
        first, second = idx[a * CAP, owner], idx[a * CAP + 1, owner]
        values = []
        for lb in range(blocks):
            total = None
            for c in range(comps):
                s0 = jnp.broadcast_to(strain[c, lb, pl.ds(first, 1), :], upper.shape)
                s1 = jnp.broadcast_to(strain[c, lb, pl.ds(second, 1), :], upper.shape)
                term = w[a, c] * jnp.where(upper, s0, s1)
                total = term if total is None else total + term
            values.append(total)
        return jnp.concatenate(values, axis=1)

    def send_group(a, m):
        for k in range(1, nd):
            dk = lax.rem(d + k, nd)
            for sign in range(2):
                ysend[a, m, k - 1, sign] = pair(a, dest_z(m, sign) * nd + dk)
            remote(
                ysend.at[a, m, k - 1], yrecv.at[a, m, d], y_ss.at[a, m], y_rs.at[a, m], plane(k)
            ).start()
        for sign in range(2):
            yrecv[a, m, d, sign] = pair(a, dest_z(m, sign) * nd + d)

    def need_group(a, m):
        wait_bytes(yrecv.at[a, m, pl.ds(0, nd - 1)], y_rs.at[a, m])

    def work(a, m, sign, g):
        zd = dest_z(m, sign)
        lhs = ohm[a, pl.ds(pl.multiple_of(zd * ROWS, ROWS), ROWS), :].astype(bf16)
        values = []
        for i in range(per):
            p = yrecv[a, m, :, sign].reshape(nd * 2 * QDIR, px)
            e = jnp.exp2(p * (ra[g * per + i] * (2.0 * scale) - p))
            hi = e.astype(bf16)
            lo = (e - hi.astype(f32)).astype(bf16)
            values.append(jnp.dot(lhs, jnp.concatenate([hi, lo], axis=0), preferred_element_type=f32))
        return values

    def z_step(a, m, g, way, has):
        here = zrecv.at[a, m - 1, way, g]
        values = work(a, m, way, g)
        if has:
            wait_bytes(here, z_rs.at[a, m - 1, way, g])
            values = [value + here[i] for i, value in enumerate(values)]
        for i, value in enumerate(values):
            here[i] = value
        remote(
            here, zrecv.at[a, m, way, g], z_ss.at[a, m, way, g], z_rs.at[a, m, way, g], ring(1 - 2 * way)
        ).start()

    def z_first(a):
        def go(g, carry):
            for way in range(2):
                at = g + way * GROUPS // 2
                for i, value in enumerate(work(a, 0, 0, at)):
                    zfirst[a, at, i] = value
                remote(
                    zfirst.at[a, at], zrecv.at[a, 0, way, at], z_ss.at[a, 0, way, at], z_rs.at[a, 0, way, at],
                    ring(1 - 2 * way),
                ).start()
            return carry

        lax.fori_loop(0, GROUPS // 2, go, 0)

    def z_second(a):
        for has in (False, True):

            def go(i, carry, has=has):
                for way in range(2):
                    g = i + (way if has else 1 - way) * (GROUPS // 2)
                    z_step(a, 1, g, way, has)
                return carry

            lax.fori_loop(0, GROUPS // 2, go, 0)

    def z_rest(a, m):
        def go(i, carry):
            for way in range(2):
                z_step(a, m, i, way, True)
            return carry

        lax.fori_loop(0, GROUPS, go, 0)

    def finish(a, g):
        values = work(a, 0, 1, g)
        for way in range(2):
            wait_bytes(zrecv.at[a, half - 1, way, g], z_rs.at[a, half - 1, way, g])
        for i, value in enumerate(values):
            angle = jnp.full((ROWS, px), ra[g * per + i]) * scale
            value = value + zrecv[a, half - 1, 0, g, i] + zrecv[a, half - 1, 1, g, i]
            ximg[a, g, x, i] = value * (jnp.exp2(-angle * angle) * norm)
        for way in range(2):
            remote(
                ximg.at[a, g, x], ximg.at[a, g, x], x_ss.at[a, g, way], x_rs.at[a, g, way], across(1 - 2 * way)
            ).start()

    def halves(a, g, at, way):
        return ximg.at[a, g, at, pl.ds(way * (per // 2), per // 2)]

    def forward(a, g):
        for way in range(2):
            at = lax.rem(x + nx - 1 + 2 * way, nx)
            wait_bytes(ximg.at[a, g, at], x_rs.at[a, g, way])
            part = halves(a, g, at, way)
            remote(part, part, x_ss.at[a, g, 2 + way], x_rs.at[a, g, 2 + way], across(1 - 2 * way)).start()

    def resolve(a, g):
        for way in range(2):
            wait_bytes(halves(a, g, lax.rem(x + 2, nx), way), x_rs.at[a, g, 2 + way])
        total = None
        for j in range(nx):
            image = ximg[a, g, j].reshape(per * ROWS, px)
            hi = image.astype(bf16)
            lo = (image - hi.astype(f32)).astype(bf16)
            both = jnp.dot(
                jnp.concatenate([hi, lo], axis=0), res[pl.ds(j * px, px), :], preferred_element_type=f32
            )
            part = both[: per * ROWS] + both[per * ROWS :]
            total = part if total is None else total + part
        out[a, pl.ds(g * per, per)] = total.reshape(per, ROWS, res.shape[1])

    def each(fn, a):
        def go(g, carry):
            fn(a, g)
            return carry

        lax.fori_loop(0, GROUPS, go, 0)

    lead = min(LEAD, half)

    def ahead_of(a, m):
        ahead = a * half + m + lead

        @pl.when(ahead < ANGLES * half)
        def _():
            send_group(lax.div(ahead, half), lax.rem(ahead, half))

    def early(t, carry):
        send_group(0, t)
        return carry

    lax.fori_loop(0, lead, early, 0)
    wait_bytes(ohrecv.at[pl.ds(0, nd - 1)], oh_rs)
    for a in range(ANGLES):
        columns = ohrecv[:, a].reshape(nd * 2 * QDIR, nz * ROWS)
        rows = columns.T
        ohm[a] = jnp.concatenate([rows, rows], axis=1)

    def steady(a):
        def go(m, carry):
            ahead_of(a, m)
            need_group(a, m)
            z_rest(a, m)
            return carry

        return go

    for a in range(ANGLES):
        for m in range(2):
            ahead_of(a, m)
            need_group(a, m)
            (z_first if m == 0 else z_second)(a)
        if a > 0:
            each(finish, a - 1)
        lax.fori_loop(2, half - 1, steady(a), 0)
        if a > 0:
            each(forward, a - 1)
        if half > 2:
            lax.fori_loop(half - 1, half, steady(a), 0)
        if a > 0:
            load_res.wait()
            each(resolve, a - 1)
    last = ANGLES - 1
    finish(last, 0)

    def tail(g, carry):
        finish(last, g)
        forward(last, g - 1)
        return carry

    lax.fori_loop(1, GROUPS, tail, 0)
    forward(last, GROUPS - 1)
    each(resolve, last)

    wait_bytes(ohrecv.at[pl.ds(0, nd - 1)], oh_ss)

    def drain(t, carry):
        a, m = lax.div(t, half), lax.rem(t, half)
        wait_bytes(ysend.at[a, m, pl.ds(0, nd - 1)], y_ss.at[a, m])
        return carry

    lax.fori_loop(0, ANGLES * half, drain, 0)
    for a in range(ANGLES):

        def drain_z(m, carry):
            for way in range(2):
                for g in range(GROUPS):
                    wait_bytes(zrecv.at[a, m, way, g], z_ss.at[a, m, way, g])
            return carry

        for way in range(2):
            for g in range(way * GROUPS // 2, (way + 1) * GROUPS // 2):
                wait_bytes(zrecv.at[a, 0, way, g], z_ss.at[a, 0, way, g])
        lax.fori_loop(1, half, drain_z, 0)
        for g in range(GROUPS):
            for way in range(2):
                wait_bytes(ximg.at[a, g, 0], x_ss.at[a, g, way])
                wait_bytes(halves(a, g, 0, way), x_ss.at[a, g, 2 + way])


def local(plane, strain, dest, det_row, dirs, rock_angles, resolution):
    nslab, nx = lax.axis_size("slab"), lax.axis_size("rock")
    nd, nz = plane, nslab // plane
    half = nz // 2
    tiles, comps, px = strain.shape
    out_px = resolution.shape[1]
    rocks = rock_angles.shape[0]
    per = rocks // GROUPS
    lanes = min(128, px)
    blocks = px // lanes
    norm = ROWS / (QDIR * DEPTH * TILES_DEV)

    smem = pl.BlockSpec(memory_space=pltpu.SMEM)
    vmem = pl.BlockSpec(memory_space=pltpu.VMEM)
    hbm = pl.BlockSpec(memory_space=pl.ANY)
    dma = pltpu.SemaphoreType.DMA
    f32 = jnp.float32
    image = (per, ROWS, px)
    resolved = pl.pallas_call(
        functools.partial(kernel, nz, nd, norm),
        out_shape=jax.ShapeDtypeStruct((ANGLES, rocks, ROWS, out_px), f32),
        in_specs=[smem, smem, vmem, vmem, hbm, hbm],
        out_specs=vmem,
        scratch_shapes=[
            pltpu.SMEM((ANGLES * CAP, nslab), jnp.int32),
            pltpu.VMEM((ANGLES * CAP, nslab), jnp.int32),
            pltpu.VMEM((ANGLES, comps, 2 * QDIR, lanes), f32),
            pltpu.VMEM((comps, blocks, tiles, lanes), f32),
            pltpu.VMEM(resolution.shape, resolution.dtype),
            pltpu.VMEM((nd, ANGLES, CAP * QDIR, nz * ROWS), f32),
            pltpu.VMEM((ANGLES, half, nd - 1, 2, 2 * QDIR, px), f32),
            pltpu.VMEM((ANGLES, half, nd, 2, 2 * QDIR, px), f32),
            pltpu.VMEM((nd, ANGLES, CAP * QDIR, nz * ROWS), f32),
            pltpu.VMEM((ANGLES, nz * ROWS, 2 * nd * 2 * QDIR), f32),
            pltpu.VMEM((ANGLES, GROUPS, *image), f32),
            pltpu.VMEM((ANGLES, half, 2, GROUPS, *image), f32),
            pltpu.VMEM((ANGLES, GROUPS, nx, *image), f32),
            dma((comps * blocks + 1,)),
            dma,
            dma,
            dma,
            dma((ANGLES, half)),
            dma((ANGLES, half)),
            dma((ANGLES, half, 2, GROUPS)),
            dma((ANGLES, half, 2, GROUPS)),
            dma((ANGLES, GROUPS, 4)),
            dma((ANGLES, GROUPS, 4)),
        ],
        compiler_params=pltpu.CompilerParams(collective_id=0, has_side_effects=True),
    )(
        rock_angles,
        dirs,
        dest.reshape(ANGLES, tiles),
        det_row,
        jnp.transpose(strain, (1, 0, 2)),
        resolution,
    )
    return jnp.swapaxes(resolved, 1, 2)


def solution(mesh):
    placed = (
        P("slab", None, "rock"),
        P(None, "slab", None),
        P(None, "slab"),
        P(),
        P(),
        P(None, "rock"),
    )
    return jax.shard_map(
        functools.partial(local, PLANE),
        mesh=mesh,
        in_specs=placed,
        out_specs=P(None, "slab", None, "rock"),
        check_vma=False,
    )
```

```python
import functools
import math

import jax
import jax.numpy as jnp
from jax import lax
from jax.experimental import pallas as pl
from jax.experimental.pallas import tpu as pltpu
from jax.sharding import PartitionSpec as P

TILES_DEV = 128
DEPTH = 1
QDIR = 4
ROWS = 8
ANGLES = 2
CAP = 2
PLANE = 8
GROUPS = 4
LEAD = 11
MESH = pl.DeviceIdType.MESH


def kernel(
    nz, nd, norm,
    ra, dirs, dest, det_row, strain_hbm, res_hbm, out,
    idx, idx_v, w, strain, res, oh, ysend, yrecv, ohrecv, ohm, zleaf, zown, zoh, zrecv, ximg, summed,
    load_s, idx_s, oh_ss, oh_rs, y_ss, y_rs, p_ss, p_rs, z_ss, z_rs, x_ss, x_rs,
):
    me = lax.axis_index("slab")
    x = lax.axis_index("rock")
    nx = 4
    z = lax.div(me, nd)
    d = lax.rem(me, nd)
    half = nz // 2
    owners = nz * nd
    comps, blocks, tiles, lanes = strain.shape
    px = blocks * lanes
    per = zrecv.shape[4]
    hp = px // 2
    scale = math.sqrt(0.5 * math.log2(math.e))
    f32, i32, bf16 = jnp.float32, jnp.int32, jnp.bfloat16

    def plane(k):
        return {"slab": z * nd + lax.rem(d + k, nd)}

    def ring(step):
        return {"slab": lax.rem(z + step + nz, nz) * nd + d}

    def across(k):
        return {"rock": lax.rem(x + k + nx, nx)}

    def remote(src, dst, ss, rs, peer):
        return pltpu.make_async_remote_copy(
            src_ref=src, dst_ref=dst, send_sem=ss, recv_sem=rs, device_id=peer, device_id_type=MESH
        )

    def wait_bytes(ref, sem):
        pltpu.make_async_copy(ref, ref, sem).wait()

    peers = [plane(k) for k in range(1, nd)] + [ring(1), ring(-1), across(1), across(-1)]
    barrier = pltpu.get_barrier_semaphore()
    for peer in peers:
        pl.semaphore_signal(barrier, inc=1, device_id=peer, device_id_type=MESH)

    loads = [
        pltpu.make_async_copy(
            strain_hbm.at[c, :, pl.ds(lb * lanes, lanes)], strain.at[c, lb], load_s.at[c * blocks + lb]
        )
        for c in range(comps)
        for lb in range(blocks)
    ]
    for load in loads:
        load.start()
    load_res = pltpu.make_async_copy(res_hbm, res, load_s.at[comps * blocks])

    upper = lax.broadcasted_iota(i32, (2 * QDIR, lanes), 0) < QDIR
    upper_rows = lax.broadcasted_iota(i32, (2 * QDIR, owners), 0) < QDIR
    number = lax.broadcasted_iota(i32, (tiles, owners), 0)
    owner_of = lax.broadcasted_iota(i32, (tiles, owners), 1)
    slot_rows = []
    for a in range(ANGLES):
        named = jnp.broadcast_to(dest[pl.ds(a, 1), :].astype(f32), (owners, tiles)).T.astype(i32)
        falls = jnp.broadcast_to(det_row[pl.ds(a, 1), :].astype(f32), (owners, tiles)).T.astype(i32)
        key = number * ROWS + falls
        match = named == owner_of
        low = jnp.min(jnp.where(match, key, tiles * ROWS), axis=0, keepdims=True)
        high = jnp.max(jnp.where(match, key, -1), axis=0, keepdims=True)
        low = jnp.where(high >= 0, low, -1)
        high = jnp.where(high > low, high, -1)
        for slot, keys in enumerate((low, high)):
            idx_v[pl.ds(a * CAP + slot, 1), :] = lax.shift_right_logical(jnp.maximum(keys, 0), 3)
        low, high = [jnp.where(keys >= 0, keys & (ROWS - 1), -1).astype(f32) for keys in (low, high)]
        slot_rows.append(
            jnp.where(upper_rows, jnp.broadcast_to(low, upper_rows.shape), jnp.broadcast_to(high, upper_rows.shape))
        )
    idx_copy = pltpu.make_async_copy(idx_v, idx, idx_s)
    idx_copy.start()
    slot_rows = jnp.concatenate(slot_rows, axis=0).astype(bf16)
    source = lax.broadcasted_iota(i32, (owners, nz * ROWS), 0)
    target = lax.broadcasted_iota(i32, (owners, nz * ROWS), 1)
    row_of = (lax.broadcasted_iota(i32, (2 * ANGLES * QDIR, nz * ROWS), 1) & (ROWS - 1)).astype(f32)
    start_of = lax.shift_right_logical(target, 3) * nd
    for k in range(nd):
        spread = jnp.where(source == start_of + k, 1.0, 0.0).astype(bf16)
        there = jnp.dot(slot_rows, spread, preferred_element_type=f32)
        hot = jnp.where(there == row_of, 1.0, 0.0)
        for a in range(ANGLES):
            oh[k, a] = hot[a * 2 * QDIR : (a + 1) * 2 * QDIR]
    qs = lax.broadcasted_iota(i32, (2 * QDIR, lanes), 0) & (QDIR - 1)
    for a in range(ANGLES):
        for c in range(comps):
            column = jnp.full(qs.shape, dirs[a, 0, c])
            for q in range(1, QDIR):
                column = jnp.where(qs == q, dirs[a, q, c], column)
            w[a, c] = column * scale
    idx_copy.wait()
    for load in loads:
        load.wait()

    for a in range(ANGLES):
        summed[a] = jnp.zeros(summed.shape[1:], f32)

    def dest_z(m, sign):
        return lax.rem(z + (half - m) * (1 - 2 * sign) + nz, nz)

    pl.semaphore_wait(barrier, len(peers))

    for k in range(1, nd):
        remote(oh.at[lax.rem(d + k, nd)], ohrecv.at[d], oh_ss, oh_rs, plane(k)).start()
    ohrecv[d] = oh[d]

    def pair(a, owner):
        first, second = idx[a * CAP, owner], idx[a * CAP + 1, owner]
        values = []
        for lb in range(blocks):
            total = None
            for c in range(comps):
                s0 = jnp.broadcast_to(strain[c, lb, pl.ds(first, 1), :], upper.shape)
                s1 = jnp.broadcast_to(strain[c, lb, pl.ds(second, 1), :], upper.shape)
                term = w[a, c] * jnp.where(upper, s0, s1)
                total = term if total is None else total + term
            values.append(total)
        return jnp.concatenate(values, axis=1)

    def unit(n):
        first = n < 3 * ANGLES
        rest = jnp.maximum(n - 3 * ANGLES, 0)
        a = jnp.where(first, lax.div(n, 3), lax.div(rest, nz - 3))
        v = jnp.where(first, lax.rem(n, 3) + 1, lax.rem(rest, nz - 3) + 4)
        return a, lax.div(v, 2), lax.rem(v, 2)

    def send_part(n, k):
        a, m, sign = unit(n)
        there = ysend.at[a, m, sign, k]
        there[...] = pair(a, dest_z(m, sign) * nd + lax.rem(d + k, nd))

        @pl.when(k > 0)
        def _():
            remote(there, yrecv.at[a, m, sign, d], y_ss.at[a, m, sign], y_rs.at[a, m, sign], plane(k)).start()

        @pl.when(k == 0)
        def _():
            pltpu.make_async_copy(there, yrecv.at[a, m, sign, d], y_rs.at[a, m, sign]).start()

    def advance(t, i):
        for j in range(2):
            n = LEAD + 2 * t + j

            @pl.when(n < ANGLES * nz)
            def _():
                for k in range(nd // GROUPS):
                    send_part(n, i * (nd // GROUPS) + k)

    def need(a, m, sign):
        wait_bytes(yrecv.at[a, m, sign], y_rs.at[a, m, sign])

    def lines(a, zd):
        return ohm.at[a, pl.ds(pl.multiple_of(zd * ROWS, ROWS), ROWS), :]

    def images(p_ref, hot, g):
        lhs = hot[...].astype(bf16)
        values = []
        for i in range(per):
            p = p_ref[...].reshape(nd * 2 * QDIR, p_ref.shape[-1])
            e = jnp.exp2(p * (ra[g * per + i] * (2.0 * scale) - p))
            hi = e.astype(bf16)
            lo = (e - hi.astype(f32)).astype(bf16)
            values.append(jnp.dot(lhs, jnp.concatenate([hi, lo], axis=0), preferred_element_type=f32))
        return values

    def work(a, m, sign, g):
        return images(yrecv.at[a, m, sign], lines(a, dest_z(m, sign)), g)

    def pass_on(a, way, kind, pairs):
        for j, (src, dst) in enumerate(pairs):
            remote(src, dst, p_ss.at[a, kind + j, way], p_rs.at[a, kind + j, way], ring(1 - 2 * way)).start()

    def leaf(a):
        need(a, 0, 1)
        for way in range(2):
            part = yrecv.at[a, 0, 1, :, :, pl.ds(way * hp, hp)]
            pass_on(a, way, 0, [(part, zleaf.at[a, 0, way]), (lines(a, dest_z(0, 1)), zoh.at[a, 0, way])])

    def second(a):
        need(a, 1, 0)
        need(a, 1, 1)
        for way in range(2):
            pass_on(
                a, way, 2,
                [(yrecv.at[a, 1, way], zown.at[a, way]), (lines(a, dest_z(1, way)), zoh.at[a, 1, way])],
            )

    def leaf_again(a):
        for way in range(2):
            wait_bytes(zleaf.at[a, 0, way], p_rs.at[a, 0, way])
            wait_bytes(zoh.at[a, 0, way], p_rs.at[a, 1, way])
            pass_on(
                a, way, 4, [(zleaf.at[a, 0, way], zleaf.at[a, 1, way]), (zoh.at[a, 0, way], zoh.at[a, 2, way])]
            )

    def send_on(a, m, g, way, values):
        here = zrecv.at[a, m - 1, way, g]
        for i, value in enumerate(values):
            here[i] = value
        remote(
            here, zrecv.at[a, m, way, g], z_ss.at[a, m, way, g], z_rs.at[a, m, way, g], ring(1 - 2 * way)
        ).start()

    def z_third(a):
        def go(g, carry):
            advance(a * (half - 2), g)
            for way in range(2):
                values = work(a, 2, way, g)
                if_first = [(zown.at[a, way], 2), (zoh.at[a, 1, way], 3), (zleaf.at[a, 1, way], 4), (zoh.at[a, 2, way], 5)]

                @pl.when(g == 0)
                def _():
                    for ref, kind in if_first:
                        wait_bytes(ref, p_rs.at[a, kind, way])

                near = images(zown.at[a, way], zoh.at[a, 1, way], g)
                far = images(zleaf.at[a, 1, way], zoh.at[a, 2, way], g)
                total = []
                for one, two, three in zip(values, near, far):
                    sides = [one[:, :hp] + two[:, :hp], one[:, hp:] + two[:, hp:]]
                    sides[way] = sides[way] + three
                    total.append(jnp.concatenate(sides, axis=1))
                send_on(a, 2, g, way, total)
            return carry

        lax.fori_loop(0, GROUPS, go, 0)

    def z_step(a, m, g, way):
        here = zrecv.at[a, m - 1, way, g]
        values = work(a, m, way, g)
        wait_bytes(here, z_rs.at[a, m - 1, way, g])
        send_on(a, m, g, way, [value + here[i] for i, value in enumerate(values)])

    def z_rest(a, m, extra=None):
        def go(i, carry):
            advance(a * (half - 2) + m - 2, i)
            for way in range(2):
                z_step(a, m, i, way)
            if extra is not None:
                extra(i)
            return carry

        lax.fori_loop(0, GROUPS, go, 0)

    def finish(a, g):
        values = work(a, half, 0, g)
        for way in range(2):
            wait_bytes(zrecv.at[a, half - 1, way, g], z_rs.at[a, half - 1, way, g])
        for i, value in enumerate(values):
            angle = jnp.full((ROWS, px), ra[g * per + i]) * scale
            value = value + zrecv[a, half - 1, 0, g, i] + zrecv[a, half - 1, 1, g, i]
            ximg[a, g, x, i] = value * (jnp.exp2(-angle * angle) * norm)
        for way in range(2):
            remote(
                ximg.at[a, g, x], ximg.at[a, g, x], x_ss.at[a, g, way], x_rs.at[a, g, way], across(1 - 2 * way)
            ).start()

    def halves(a, g, at, way):
        return ximg.at[a, g, at, pl.ds(way * (per // 2), per // 2)]

    def forward(a, g):
        for way in range(2):
            at = lax.rem(x + nx - 1 + 2 * way, nx)
            wait_bytes(ximg.at[a, g, at], x_rs.at[a, g, way])
            part = halves(a, g, at, way)
            remote(part, part, x_ss.at[a, g, 2 + way], x_rs.at[a, g, 2 + way], across(1 - 2 * way)).start()

    def split(image):
        hi = image.astype(bf16)
        return jnp.concatenate([hi, (image - hi.astype(f32)).astype(bf16)], axis=0)

    def far(a, g):
        for way in range(2):
            wait_bytes(halves(a, g, lax.rem(x + 2, nx), way), x_rs.at[a, g, 2 + way])

    def columns_of(j):
        return res[pl.ds(pl.multiple_of(j * px, px), px), :]

    def resolve_block(a, j):
        rows = per * GROUPS * ROWS
        both = jnp.dot(split(ximg[a, :, j].reshape(rows, px)), columns_of(j), preferred_element_type=f32)
        part = both[:rows] + both[rows:]
        for lb in range(blocks):
            summed[a, lb] += part[:, lb * lanes : (lb + 1) * lanes]

    def resolve_group(a, g):
        rows = per * ROWS
        total = None
        for k in (0, 1, 3, 2):
            j = lax.rem(x + k, nx)
            if k == 2:
                far(a, g)
            both = jnp.dot(split(ximg[a, g, j].reshape(rows, px)), columns_of(j), preferred_element_type=f32)
            part = both[:rows] + both[rows:]
            total = part if total is None else total + part
        for lb in range(blocks):
            summed[a, lb, pl.ds(pl.multiple_of(g * rows, rows), rows), :] = total[:, lb * lanes : (lb + 1) * lanes]

    def deliver(a):
        for row in range(ROWS):
            for lb in range(blocks):
                out[a, row, :, pl.ds(lb * lanes, lanes)] = summed[a, lb, pl.ds(row, per * GROUPS, stride=ROWS), :]

    def each(fn, a):
        def go(g, carry):
            fn(a, g)
            return carry

        lax.fori_loop(0, GROUPS, go, 0)

    def early(n, carry):
        def go(k, inner):
            send_part(n, k)
            return inner

        lax.fori_loop(0, nd, go, 0)
        return carry

    lax.fori_loop(0, 3, early, 0)
    load_res.start()
    wait_bytes(ohrecv.at[pl.ds(0, nd - 1)], oh_rs)
    for a in range(ANGLES):
        columns = ohrecv[:, a].reshape(nd * 2 * QDIR, nz * ROWS)
        rows = columns.T
        ohm[a] = jnp.concatenate([rows, rows], axis=1)

    def steady(a, extra=None):
        def go(m, carry):
            need(a, m, 0)
            need(a, m, 1)
            z_rest(a, m, extra)
            return carry

        return go

    leaf(0)
    lax.fori_loop(3, 6, early, 0)
    second(0)
    lax.fori_loop(6, 8, early, 0)
    leaf_again(0)
    leaf(1)
    lax.fori_loop(8, LEAD, early, 0)
    second(1)
    leaf_again(1)
    cut = half // 2
    for a in range(ANGLES):
        need(a, 2, 0)
        need(a, 2, 1)
        z_third(a)
        if a > 0:
            need(a - 1, half, 0)
            each(finish, a - 1)
        lax.fori_loop(3, cut, steady(a), 0)
        if a > 0:
            each(forward, a - 1)
            load_res.wait()
        lax.fori_loop(cut, half - 2, steady(a), 0)
        extra = None
        if a > 0:
            each(far, a - 1)
            extra = lambda j, a=a: resolve_block(a - 1, j)
        lax.fori_loop(half - 2, half - 1, steady(a, extra), 0)
        lax.fori_loop(half - 1, half, steady(a), 0)
        if a > 0:
            deliver(a - 1)
    last = ANGLES - 1
    need(last, half, 0)
    finish(last, 0)

    def tail(g, carry):
        finish(last, g)
        forward(last, g - 1)
        return carry

    lax.fori_loop(1, GROUPS, tail, 0)
    resolve_group(last, 0)
    forward(last, GROUPS - 1)

    def rest(g, carry):
        resolve_group(last, g)
        return carry

    lax.fori_loop(1, GROUPS, rest, 0)
    deliver(last)

    wait_bytes(ohrecv.at[pl.ds(0, nd - 1)], oh_ss)

    def drain(n, carry):
        a, m, sign = unit(n)
        wait_bytes(ysend.at[a, m, sign, pl.ds(0, nd - 1)], y_ss.at[a, m, sign])
        return carry

    lax.fori_loop(0, ANGLES * nz, drain, 0)
    for a in range(ANGLES):

        def drain_z(m, carry):
            for way in range(2):
                for g in range(GROUPS):
                    wait_bytes(zrecv.at[a, m, way, g], z_ss.at[a, m, way, g])
            return carry

        for way in range(2):
            for kind, ref in enumerate(
                (zleaf.at[a, 0, way], zoh.at[a, 0, way], zown.at[a, way], zoh.at[a, 0, way], zleaf.at[a, 0, way], zoh.at[a, 0, way])
            ):
                wait_bytes(ref, p_ss.at[a, kind, way])
        lax.fori_loop(2, half, drain_z, 0)
        for g in range(GROUPS):
            for way in range(2):
                wait_bytes(ximg.at[a, g, 0], x_ss.at[a, g, way])
                wait_bytes(halves(a, g, 0, way), x_ss.at[a, g, 2 + way])


def local(plane, strain, dest, det_row, dirs, rock_angles, resolution):
    nslab, nx = lax.axis_size("slab"), lax.axis_size("rock")
    nd, nz = plane, nslab // plane
    half = nz // 2
    tiles, comps, px = strain.shape
    out_px = resolution.shape[1]
    rocks = rock_angles.shape[0]
    per = rocks // GROUPS
    lanes = min(128, px)
    blocks = px // lanes
    norm = ROWS / (QDIR * DEPTH * TILES_DEV)

    smem = pl.BlockSpec(memory_space=pltpu.SMEM)
    vmem = pl.BlockSpec(memory_space=pltpu.VMEM)
    hbm = pl.BlockSpec(memory_space=pl.ANY)
    dma = pltpu.SemaphoreType.DMA
    f32 = jnp.float32
    image = (per, ROWS, px)
    resolved = pl.pallas_call(
        functools.partial(kernel, nz, nd, norm),
        out_shape=jax.ShapeDtypeStruct((ANGLES, ROWS, rocks, out_px), f32),
        in_specs=[smem, smem, vmem, vmem, hbm, hbm],
        out_specs=vmem,
        scratch_shapes=[
            pltpu.SMEM((ANGLES * CAP, nslab), jnp.int32),
            pltpu.VMEM((ANGLES * CAP, nslab), jnp.int32),
            pltpu.VMEM((ANGLES, comps, 2 * QDIR, lanes), f32),
            pltpu.VMEM((comps, blocks, tiles, lanes), f32),
            pltpu.VMEM(resolution.shape, resolution.dtype),
            pltpu.VMEM((nd, ANGLES, CAP * QDIR, nz * ROWS), f32),
            pltpu.VMEM((ANGLES, half + 1, 2, nd, 2 * QDIR, px), f32),
            pltpu.VMEM((ANGLES, half + 1, 2, nd, 2 * QDIR, px), f32),
            pltpu.VMEM((nd, ANGLES, CAP * QDIR, nz * ROWS), f32),
            pltpu.VMEM((ANGLES, nz * ROWS, 2 * nd * 2 * QDIR), f32),
            pltpu.VMEM((ANGLES, 2, 2, nd, 2 * QDIR, px // 2), f32),
            pltpu.VMEM((ANGLES, 2, nd, 2 * QDIR, px), f32),
            pltpu.VMEM((ANGLES, 3, 2, ROWS, 2 * nd * 2 * QDIR), f32),
            pltpu.VMEM((ANGLES, half, 2, GROUPS, *image), f32),
            pltpu.VMEM((ANGLES, GROUPS, nx, *image), f32),
            pltpu.VMEM((ANGLES, blocks, rocks * ROWS, lanes), f32),
            dma((comps * blocks + 1,)),
            dma,
            dma,
            dma,
            dma((ANGLES, half + 1, 2)),
            dma((ANGLES, half + 1, 2)),
            dma((ANGLES, 6, 2)),
            dma((ANGLES, 6, 2)),
            dma((ANGLES, half, 2, GROUPS)),
            dma((ANGLES, half, 2, GROUPS)),
            dma((ANGLES, GROUPS, 4)),
            dma((ANGLES, GROUPS, 4)),
        ],
        compiler_params=pltpu.CompilerParams(collective_id=0, has_side_effects=True),
    )(
        rock_angles,
        dirs,
        dest.reshape(ANGLES, tiles),
        det_row,
        jnp.transpose(strain, (1, 0, 2)),
        resolution,
    )
    return resolved


def solution(mesh):
    placed = (
        P("slab", None, "rock"),
        P(None, "slab", None),
        P(None, "slab"),
        P(),
        P(),
        P(None, "rock"),
    )
    return jax.shard_map(
        functools.partial(local, PLANE),
        mesh=mesh,
        in_specs=placed,
        out_specs=P(None, "slab", None, "rock"),
        check_vma=False,
    )
```
